32 devices in a mesh: layer: 8 (over z, x), land: 4 (over y, core).
Axes of the slice: x: 2, y: 2, z: 4, core: 2. Of those that a mesh axis runs over, the one named last changes fastest.
Arguments:
- gradients: bfloat16 [960, 65536], P(None, ('layer', 'land')), may hold values from -6 to 6
- queries: bfloat16 [32, 65536], P(None, ('layer', 'land')), may hold values from -6 to 6
- landmarks: bfloat16 [1024, 65536], P(None, ('layer', 'land')), may hold values from -0.0234375 to 0.0234375
- whitening: bfloat16 [1024, 1024], P(None, 'land'), may hold values from -2.5 to 2.5
Outputs:
- scores: float32 [32, 960], P('land', 'layer')
The draws below stay inside these ranges and needn't reach their ends.
All inputs are finite; a program needn't handle non-finite values.
Results may differ from the reference program's by a relative error of at most 0.023.
Values may be sent and summed in bfloat16 or wider, within the bound.
A program may use at most 128 MiB of HBM per device.

```python
import math
import jax
import jax.numpy as jnp

LANDMARKS = 1024
FEAT = 65536
ROWS = 960
NQ = 32


def draw_whitening(key, part):
    key_diag, key_off = jax.random.split(key)
    diagonal = jnp.exp(jax.random.uniform(key_diag, (LANDMARKS,), jnp.float32, math.log(0.5), math.log(2.0)))
    offdiag = jax.random.normal(key_off, (LANDMARKS, LANDMARKS), jnp.float32) * (0.6 / math.sqrt(LANDMARKS))
    identity = jnp.eye(LANDMARKS, dtype=jnp.float32)
    return (offdiag + identity * diagonal[None, :]).astype(jnp.bfloat16)


def block_levels(own_key, shape, pieces, low, top_value):
    factor_of = 1.0
    for axis_at, blocks in pieces:
        steps = jax.random.uniform(jax.random.fold_in(jax.random.fold_in(own_key, 6), axis_at), (blocks,), jnp.float32, low / len(pieces), top_value / len(pieces))
        factor_of = factor_of * jnp.repeat(jnp.exp(steps), shape[axis_at] // blocks).reshape((-1,) + (1,) * (len(shape) - 1 - axis_at))
    return factor_of


def noise(stream_key, dims, spread, limit, pieces=(), kind=jnp.bfloat16):
    drawn = spread * jax.random.normal(stream_key, dims, jnp.float32)
    if pieces:
        drawn = drawn * block_levels(stream_key, dims, pieces, -0.22, 0.18)
    return jnp.clip(drawn, -limit, limit).astype(kind)


def setup_inputs(seed: int = 0) -> dict:
    seeds = jax.random.split(jax.random.key(seed), 5)
    return {
        "gradients": noise(seeds[0], (ROWS, FEAT), 1.0, 6.0, ((1, 32),)),
        "queries": noise(seeds[1], (NQ, FEAT), 1.0, 6.0, ((1, 32),)),
        "landmarks": noise(seeds[2], (LANDMARKS, FEAT), FEAT ** -0.5, 0.0234375, ((1, 32),)),
        "whitening": draw_whitening(jax.random.fold_in(seeds[4], 71), 0),
    }


def reference(gradients, queries, landmarks, whitening):
    projected = jnp.dot(gradients, landmarks.T, preferred_element_type=jnp.float32).astype(jnp.bfloat16)
    query_proj = jnp.dot(queries, landmarks.T, preferred_element_type=jnp.float32).astype(jnp.bfloat16)
    whitened = jnp.dot(projected, whitening, preferred_element_type=jnp.float32).astype(jnp.bfloat16)
    query_white = jnp.dot(query_proj, whitening, preferred_element_type=jnp.float32).astype(jnp.bfloat16)
    scores = jnp.dot(query_white, whitened.T, preferred_element_type=jnp.float32)
    return scores * (LANDMARKS ** -0.5)
```

```python
import functools
import jax
import jax.numpy as jnp
from jax import lax
from jax.experimental import pallas as pl
from jax.experimental.pallas import tpu as pltpu
from jax.sharding import PartitionSpec as P

NN = (((1,), (0,)), ((), ()))
NT = (((1,), (1,)), ((), ()))
HALF = jnp.bfloat16
FULL = jnp.float32
VMEM_LIMIT = 63 << 20


def dot(a, b, dims):
    return lax.dot_general(a, b, dims, preferred_element_type=FULL)


def hub(g):
    low = lax.rem(lax.div(g, 2), 2) if not isinstance(g, int) else g // 2 % 2
    high = lax.div(g, 4) if not isinstance(g, int) else g // 4
    return g + (1 - low) * (4 - 8 * high)


def kernel(
    factor,
    g_hbm, q_hbm, l_hbm, w_hbm, out_ref,
    g_buf, p_buf, q_buf, l_buf, w_buf, load_sem,
    qs, qr, hs, hr, us, ur, bs, br, ss, sr,
    sum_send, sum_recv, land_send, land_recv,
    all_send, all_recv, score_send, score_recv, w_send, w_recv,
):
    n_layer, n_land = 8, 4
    layer = lax.axis_index("layer")
    land = lax.axis_index("land")
    core = lax.rem(land, 2)
    first = land - core
    across = lax.rem(land + 2, n_land)
    own = hub(layer)
    on_one = core == 1
    n_mark = l_buf.shape[0]
    parts = load_sem.shape[0] - 3
    span = n_mark // parts

    def span_of(b):
        return pl.ds(b * span, span)

    loads = [pltpu.make_async_copy(q_hbm, q_buf, load_sem.at[0])]
    for b in range(parts):
        loads.append(pltpu.make_async_copy(
            l_hbm.at[span_of(b)], l_buf.at[span_of(b)], load_sem.at[1 + b]))
    load_g = pltpu.make_async_copy(g_hbm, g_buf, load_sem.at[1 + parts])
    load_w = pltpu.make_async_copy(w_hbm, w_buf.at[1], load_sem.at[2 + parts])
    for load in loads:
        load.start()

    def device(to_layer, to_land):
        return dict(device_id=(to_layer, to_land), device_id_type=pl.DeviceIdType.MESH)

    def remote(source, target, send, recv, to_layer, to_land):
        return pltpu.make_async_remote_copy(
            src_ref=source, dst_ref=target, send_sem=send, recv_sem=recv,
            **device(to_layer, to_land))

    barrier = pltpu.get_barrier_semaphore()

    @pl.when(on_one)
    def _():
        for k in range(n_layer):
            for c in range(2):
                if c == 0:
                    pl.semaphore_signal(barrier, inc=1, **device(k, first))
                else:
                    @pl.when(layer != k)
                    def _():
                        pl.semaphore_signal(barrier, inc=1, **device(k, first + 1))
        pl.semaphore_signal(barrier, inc=1, **device(layer, across))

    rows = qs.shape[1]
    loads[0].wait()
    for b in range(parts):
        loads[1 + b].wait()
        if b == parts - 1:
            load_g.start()
        part = dot(q_buf[...], l_buf[b * span:(b + 1) * span, :], NT)
        for g in range(n_layer):
            qs[g, :, b * span:(b + 1) * span] = part[g * rows:(g + 1) * rows].astype(HALF)

    @pl.when(on_one)
    def _():
        load_w.start()
        qr[layer, 1] = qs[own]

    pl.semaphore_wait(barrier, n_layer)

    def sums(g):
        return remote(qs.at[g], qr.at[layer, core], sum_send.at[g],
                      sum_recv.at[layer, core], hub(g), first + 1)

    def for_sums(act):
        for g in range(n_layer):
            @pl.when(jnp.logical_or(layer != hub(g), core == 0))
            def _():
                act(sums(g))

    for_sums(lambda copy: copy.start())

    share_w = remote(w_hbm, w_buf.at[0], w_send, w_recv, layer, first + 1)

    @pl.when(core == 0)
    def _():
        share_w.start()

    each = p_buf.shape[1]
    width = 256

    def project(b):
        part = dot(g_buf[...], l_buf[b * width:(b + 1) * width, :], NT)
        for i in range(n_layer):
            p_buf[i, :, b * width:(b + 1) * width] = part[i * each:(i + 1) * each].astype(HALF)

    load_g.wait()
    project(0)
    project(1)
    project(2)

    def gathers(k, c):
        return remote(bs, br.at[own], all_send.at[k, c], all_recv.at[own], k, first + c)

    def for_gathers(act):
        for k in reversed(range(n_layer)):
            act(gathers(k, 0))

            @pl.when(layer != k)
            def _():
                act(gathers(k, 1))

    @pl.when(on_one)
    def _():
        total = jnp.zeros(hs.shape, FULL)
        for k in range(n_layer):
            for c in range(2):
                def arrive():
                    pltpu.make_async_copy(
                        qs.at[0], qr.at[k, c], sum_recv.at[k, c]).wait()
                if c == 0:
                    arrive()
                else:
                    pl.when(layer != k)(arrive)
            total += qr[k, 0].astype(FULL) + qr[k, 1].astype(FULL)

        hs[...] = total.astype(HALF)
        copy = remote(hs, hr, land_send.at[0], land_recv.at[0], layer, across)
        copy.start()
        load_w.wait()
        share_w.wait_recv()
        copy.wait_recv()
        total += hr[...].astype(FULL)

        mixed = total.astype(HALF)
        back = jnp.zeros(hs.shape, FULL)
        for c in range(2):
            white = dot(mixed, w_buf[c], NN).astype(HALF)
            back += dot(white, w_buf[c], NT)
        us[...] = back.astype(HALF)
        again = remote(us, ur, land_send.at[1], land_recv.at[1], layer, across)
        again.start()
        again.wait_recv()
        back += ur[...].astype(FULL)

        bs[...] = back.astype(HALF)
        for_gathers(lambda copy: copy.start())
        br[own] = bs[...]
        copy.wait_send()
        again.wait_send()

    project(3)
    for_sums(lambda copy: copy.wait_send())

    @pl.when(core == 0)
    def _():
        share_w.wait_send()

    for g in range(n_layer):
        @pl.when(jnp.logical_or(core == 0, layer != hub(g)))
        def _():
            pltpu.make_async_copy(bs, br.at[g], all_recv.at[g]).wait()

    folded = jnp.concatenate([br[i].astype(FULL) for i in range(n_layer)], axis=0).astype(HALF)
    share = out_ref.shape[0]

    def scores(k, b):
        return remote(ss.at[k, b], sr.at[layer, land], score_send.at[k, b],
                      score_recv.at[layer, land], k, b)

    def elsewhere(k, b):
        return jnp.logical_or(layer != k, land != b)

    for k in range(n_layer):
        block = dot(folded, p_buf[k], NT) * factor
        for b in range(n_land):
            ss[k, b] = block[b * share:(b + 1) * share].astype(HALF)
        for b in range(n_land):
            @pl.when(elsewhere(k, b))
            def _():
                scores(k, b).start()
    sr[layer, land] = ss[layer, land]

    @pl.when(on_one)
    def _():
        for_gathers(lambda copy: copy.wait_send())

    result = jnp.zeros(out_ref.shape, FULL)
    for k in range(n_layer):
        for b in range(n_land):
            @pl.when(elsewhere(k, b))
            def _():
                if k < 6:
                    scores(k, b).wait_send()
                pltpu.make_async_copy(
                    ss.at[k, b], sr.at[k, b], score_recv.at[k, b]).wait()
            result += sr[k, b].astype(FULL)
    out_ref[...] = result
    for k in range(6, n_layer):
        for b in range(n_land):
            @pl.when(elsewhere(k, b))
            def _():
                scores(k, b).wait_send()


def fused(gradients, queries, landmarks, whitening):
    n_layer = lax.axis_size("layer")
    n_land = lax.axis_size("land")
    n_rows, width = gradients.shape
    n_query = queries.shape[0]
    n_mark = landmarks.shape[0]
    parts = 2
    each, rows, share = n_rows // n_layer, n_query // n_layer, n_query // n_land
    any_space = pl.BlockSpec(memory_space=pltpu.HBM)
    return pl.pallas_call(
        functools.partial(kernel, n_mark ** (-0.5)),
        out_shape=jax.ShapeDtypeStruct((share, each), FULL),
        in_specs=[any_space] * 4,
        out_specs=pl.BlockSpec(memory_space=pltpu.VMEM),
        scratch_shapes=[
            pltpu.VMEM((n_rows, width), HALF),
            pltpu.VMEM((n_layer, each, n_mark), HALF),
            pltpu.VMEM((n_query, width), HALF),
            pltpu.VMEM((n_mark, width), HALF),
            pltpu.VMEM((2, *whitening.shape), HALF),
            pltpu.SemaphoreType.DMA((parts + 3,)),
            pltpu.VMEM((n_layer, rows, n_mark), HALF),
            pltpu.VMEM((n_layer, 2, rows, n_mark), HALF),
            pltpu.VMEM((rows, n_mark), HALF),
            pltpu.VMEM((rows, n_mark), HALF),
            pltpu.VMEM((rows, n_mark), HALF),
            pltpu.VMEM((rows, n_mark), HALF),
            pltpu.VMEM((rows, n_mark), HALF),
            pltpu.VMEM((n_layer, rows, n_mark), HALF),
            pltpu.VMEM((n_layer, n_land, share, each), HALF),
            pltpu.VMEM((n_layer, n_land, share, each), HALF),
            pltpu.SemaphoreType.DMA((n_layer,)),
            pltpu.SemaphoreType.DMA((n_layer, 2)),
            pltpu.SemaphoreType.DMA((2,)),
            pltpu.SemaphoreType.DMA((2,)),
            pltpu.SemaphoreType.DMA((n_layer, 2)),
            pltpu.SemaphoreType.DMA((n_layer,)),
            pltpu.SemaphoreType.DMA((n_layer, n_land)),
            pltpu.SemaphoreType.DMA((n_layer, n_land)),
            pltpu.SemaphoreType.DMA,
            pltpu.SemaphoreType.DMA,
        ],
        compiler_params=pltpu.CompilerParams(
            collective_id=0, has_side_effects=True, vmem_limit_bytes=VMEM_LIMIT
        ),
    )(gradients, queries, landmarks, whitening)


def staged(gradients, queries, landmarks, whitening):
    factor = landmarks.shape[0] ** (-0.5)
    partial = dot(queries, landmarks, NT).astype(HALF)
    query_proj = lax.psum(partial, ("layer", "land"))
    query_white = dot(query_proj, whitening, NN).astype(HALF)
    back = lax.psum(dot(query_white, whitening, NT).astype(HALF), "land")
    spread = dot(back, landmarks, NN).astype(HALF)
    scores = dot(spread, gradients, NT) * factor
    share = lax.psum_scatter(
        scores.astype(HALF), "layer", scatter_dimension=1, tiled=True
    )
    return lax.psum_scatter(share, "land", scatter_dimension=0, tiled=True).astype(FULL)


def local(gradients, queries, landmarks, whitening):
    held = 2 * (gradients.size + queries.size + landmarks.size + whitening.size)
    few = lax.axis_size("layer") == 8 and lax.axis_size("land") == 4
    if few and held <= (24 << 20) and gradients.shape[1] % 128 == 0:
        return fused(gradients, queries, landmarks, whitening)
    return staged(gradients, queries, landmarks, whitening)


def solution(mesh):
    return jax.shard_map(
        local,
        mesh=mesh,
        in_specs=(
            P(None, ("layer", "land")),
            P(None, ("layer", "land")),
            P(None, ("layer", "land")),
            P(None, "land"),
        ),
        out_specs=P("land", "layer"),
        check_vma=False,
    )
```

```python
import functools
import jax
import jax.numpy as jnp
from jax import lax
from jax.experimental import pallas as pl
from jax.experimental.pallas import tpu as pltpu
from jax.sharding import PartitionSpec as P

NN = (((1,), (0,)), ((), ()))
NT = (((1,), (1,)), ((), ()))
HALF = jnp.bfloat16
FULL = jnp.float32
LAYERS = 8
LANDS = 4
HUBS = 4
SPREAD = (7, 6, 1, 0, 3, 2, 5, 4)
PARTS = 8
EARLY = 2
VMEM_LIMIT = 55136 << 10


def dot(a, b, dims):
    return lax.dot_general(a, b, dims, preferred_element_type=FULL)


def hub(g):
    return (LAYERS + HUBS) // 2 - 1 - g


def kernel(
    factor,
    g_hbm, q_hbm, l_hbm, w_hbm, out_ref,
    g_buf, p_buf, q_buf, l_buf, w_buf, load_sem,
    qs, ps, qr, bs, br, fs, ss, sr,
    sum_send, sum_recv, all_send, all_recv, score_send, score_recv, pair_send, pair_recv,
    hand_send, hand_recv,
):
    n_layer, n_land, n_hub, n_side = LAYERS, LANDS, HUBS, LANDS // 2
    layer = lax.axis_index("layer")
    land = lax.axis_index("land")
    core = lax.rem(land, 2)
    side = lax.div(land, 2)
    own = hub(layer)
    on_one = core == 1
    hub_chip = jnp.logical_and(own >= 0, own < n_hub)
    is_hub = jnp.logical_and(hub_chip, on_one)
    gives_w = jnp.logical_and(hub_chip, core == 0)
    parts = load_sem.shape[0] - 3
    span = l_buf.shape[1] // parts

    loads = [pltpu.make_async_copy(q_hbm, q_buf, load_sem.at[0])]
    for b in range(parts):
        cut = pl.ds(b * span, span)
        loads.append(pltpu.make_async_copy(
            l_hbm.at[:, cut], l_buf.at[:, cut], load_sem.at[1 + b]))
    load_g = pltpu.make_async_copy(g_hbm, g_buf, load_sem.at[1 + parts])
    load_w = pltpu.make_async_copy(w_hbm, w_buf.at[1], load_sem.at[2 + parts])
    for load in loads:
        load.start()

    def device(to_layer, to_land):
        return dict(device_id=(to_layer, to_land), device_id_type=pl.DeviceIdType.MESH)

    def remote(source, target, send, recv, to_layer, to_land):
        return pltpu.make_async_remote_copy(
            src_ref=source, dst_ref=target, send_sem=send, recv_sem=recv,
            **device(to_layer, to_land))

    def elsewhere(k, b):
        return jnp.logical_or(layer != k, land != b)

    barrier = pltpu.get_barrier_semaphore()

    @pl.when(is_hub)
    def _():
        for k in range(n_layer):
            for y in range(n_side):
                @pl.when(elsewhere(k, 2 * y + 1))
                def _():
                    pl.semaphore_signal(barrier, inc=1, **device(k, 2 * y + 1))

    @pl.when(on_one)
    def _():
        pl.semaphore_signal(barrier, inc=1, **device(layer, 2 * side))

    rows = qs.shape[1]
    loads[0].wait()
    part = jnp.zeros((q_buf.shape[0], l_buf.shape[0]), FULL)
    for b in range(parts):
        loads[1 + b].wait()
        if b == parts - 1:
            load_g.start()
        cut = slice(b * span, (b + 1) * span)
        part += dot(q_buf[:, cut], l_buf[:, cut], NT)

    pair = remote(qs, ps, pair_send.at[0], pair_recv.at[0], layer, 2 * side + 1)
    share_w = remote(w_hbm, w_buf.at[0], pair_send.at[1], pair_recv.at[1], layer, 2 * side + 1)

    def sums(g, y):
        return remote(qs.at[g], qr.at[layer, side], sum_send.at[g, y],
                      sum_recv.at[layer, side], hub(g), 2 * y + 1)

    def for_sums(act):
        for g in range(n_hub):
            for y in range(n_side):
                @pl.when(elsewhere(hub(g), 2 * y + 1))
                def _():
                    act(sums(g, y))

    @pl.when(core == 0)
    def _():
        for g in range(n_hub):
            qs[g] = part[g * rows:(g + 1) * rows].astype(HALF)
        pl.semaphore_wait(barrier, 1)
        pair.start()

    pl.when(gives_w)(share_w.start)
    pl.when(is_hub)(load_w.start)

    @pl.when(on_one)
    def _():
        pair.wait_recv()
        for g in range(n_hub):
            both = part[g * rows:(g + 1) * rows] + ps[g].astype(FULL)
            qs[g] = both.astype(HALF)
        pl.semaphore_wait(barrier, n_hub * n_side - is_hub.astype(jnp.int32))
        for_sums(lambda copy: copy.start())

    @pl.when(is_hub)
    def _():
        qr[layer, side] = qs[own]

    each = p_buf.shape[1]
    width = 256

    def project(b):
        part = dot(g_buf[...], l_buf[b * width:(b + 1) * width, :], NT)
        for i in range(n_layer):
            p_buf[i, :, b * width:(b + 1) * width] = part[i * each:(i + 1) * each].astype(HALF)

    blocks = l_buf.shape[0] // width
    load_g.wait()
    for b in range(EARLY):
        project(b)

    def gathers(k, y):
        return remote(bs, br.at[own, side], all_send.at[k, y],
                      all_recv.at[own, side], k, 2 * y + 1)

    def for_gathers(act):
        for k in SPREAD:
            for y in range(n_side):
                @pl.when(elsewhere(k, 2 * y + 1))
                def _():
                    act(gathers(k, y))

    @pl.when(is_hub)
    def _():
        total = jnp.zeros(bs.shape, FULL)
        for k in range(n_layer):
            for y in range(n_side):
                @pl.when(elsewhere(k, 2 * y + 1))
                def _():
                    pltpu.make_async_copy(
                        qs.at[0], qr.at[k, y], sum_recv.at[k, y]).wait()
                total += qr[k, y].astype(FULL)
        load_w.wait()
        share_w.wait_recv()

        mixed = total.astype(HALF)
        back = jnp.zeros(bs.shape, FULL)
        for c in range(2):
            white = dot(mixed, w_buf[c], NN).astype(HALF)
            back += dot(white, w_buf[c], NT)
        bs[...] = back.astype(HALF)
        for_gathers(lambda copy: copy.start())
        br[own, side] = bs[...]

    for b in range(EARLY, blocks):
        project(b)

    pl.when(gives_w)(share_w.wait_send)
    pl.when(core == 0)(pair.wait_send)
    share = out_ref.shape[0]

    def scores(k, b):
        return remote(ss.at[k, b], sr.at[layer, land], score_send.at[k, b],
                      score_recv.at[layer, land], k, b)

    half = n_hub // 2
    for h in range(2):
        hand = remote(fs.at[h], fs.at[h], hand_send.at[h], hand_recv.at[h], layer, 2 * side)

        @pl.when(on_one)
        def _():
            pieces = []
            for g in range(h * half, (h + 1) * half):
                row = 0
                for y in range(n_side):
                    @pl.when(elsewhere(hub(g), 2 * y + 1))
                    def _():
                        pltpu.make_async_copy(bs, br.at[g, y], all_recv.at[g, y]).wait()
                    row += br[g, y].astype(FULL)
                pieces.append(row)
            fs[h] = jnp.concatenate(pieces, axis=0).astype(HALF)
            hand.start()

        pl.when(core == 0)(hand.wait_recv)
        folded = fs[h]
        for k in range(n_layer):
            block = dot(folded, p_buf[k], NT) * factor
            for b in range(2):
                ss[k, 2 * h + b] = block[b * share:(b + 1) * share].astype(HALF)
            for b in range(2 * h, 2 * h + 2):
                @pl.when(elsewhere(k, b))
                def _():
                    scores(k, b).start()
    sr[layer, land] = ss[layer, land]

    @pl.when(on_one)
    def _():
        for_sums(lambda copy: copy.wait_send())
        for h in range(2):
            remote(fs.at[h], fs.at[h], hand_send.at[h], hand_recv.at[h], layer, 2 * side).wait_send()

    @pl.when(is_hub)
    def _():
        for_gathers(lambda copy: copy.wait_send())

    result = jnp.zeros(out_ref.shape, FULL)
    for k in range(n_layer):
        for b in range(n_land):
            @pl.when(elsewhere(k, b))
            def _():
                if k < n_layer - 2:
                    scores(k, b).wait_send()
                pltpu.make_async_copy(
                    ss.at[k, b], sr.at[k, b], score_recv.at[k, b]).wait()
            result += sr[k, b].astype(FULL)
    out_ref[...] = result
    for k in range(n_layer - 2, n_layer):
        for b in range(n_land):
            @pl.when(elsewhere(k, b))
            def _():
                scores(k, b).wait_send()


def fused(gradients, queries, landmarks, whitening):
    n_layer, n_land, n_hub = LAYERS, LANDS, HUBS
    n_rows, width = gradients.shape
    n_query = queries.shape[0]
    n_mark = landmarks.shape[0]
    parts = PARTS
    each, rows, share = n_rows // n_layer, n_query // n_hub, n_query // n_land
    any_space = pl.BlockSpec(memory_space=pltpu.HBM)
    return pl.pallas_call(
        functools.partial(kernel, n_mark ** (-0.5)),
        out_shape=jax.ShapeDtypeStruct((share, each), FULL),
        in_specs=[any_space] * 4,
        out_specs=pl.BlockSpec(memory_space=pltpu.VMEM),
        scratch_shapes=[
            pltpu.VMEM((n_rows, width), HALF),
            pltpu.VMEM((n_layer, each, n_mark), HALF),
            pltpu.VMEM((n_query, width), HALF),
            pltpu.VMEM((n_mark, width), HALF),
            pltpu.VMEM((2, *whitening.shape), HALF),
            pltpu.SemaphoreType.DMA((parts + 3,)),
            pltpu.VMEM((n_hub, rows, n_mark), HALF),
            pltpu.VMEM((n_hub, rows, n_mark), HALF),
            pltpu.VMEM((n_layer, n_land // 2, rows, n_mark), HALF),
            pltpu.VMEM((rows, n_mark), HALF),
            pltpu.VMEM((n_hub, n_land // 2, rows, n_mark), HALF),
            pltpu.VMEM((2, n_query // 2, n_mark), HALF),
            pltpu.VMEM((n_layer, n_land, share, each), HALF),
            pltpu.VMEM((n_layer, n_land, share, each), HALF),
            pltpu.SemaphoreType.DMA((n_hub, n_land // 2)),
            pltpu.SemaphoreType.DMA((n_layer, n_land // 2)),
            pltpu.SemaphoreType.DMA((n_layer, n_land // 2)),
            pltpu.SemaphoreType.DMA((n_hub, n_land // 2)),
            pltpu.SemaphoreType.DMA((n_layer, n_land)),
            pltpu.SemaphoreType.DMA((n_layer, n_land)),
            pltpu.SemaphoreType.DMA((2,)),
            pltpu.SemaphoreType.DMA((2,)),
            pltpu.SemaphoreType.DMA((2,)),
            pltpu.SemaphoreType.DMA((2,)),
        ],
        compiler_params=pltpu.CompilerParams(
            collective_id=0, has_side_effects=True, vmem_limit_bytes=VMEM_LIMIT
        ),
    )(gradients, queries, landmarks, whitening)


def staged(gradients, queries, landmarks, whitening):
    factor = landmarks.shape[0] ** (-0.5)
    partial = dot(queries, landmarks, NT).astype(HALF)
    query_proj = lax.psum(partial, ("layer", "land"))
    query_white = dot(query_proj, whitening, NN).astype(HALF)
    back = lax.psum(dot(query_white, whitening, NT).astype(HALF), "land")
    spread = dot(back, landmarks, NN).astype(HALF)
    scores = dot(spread, gradients, NT) * factor
    share = lax.psum_scatter(
        scores.astype(HALF), "layer", scatter_dimension=1, tiled=True
    )
    return lax.psum_scatter(share, "land", scatter_dimension=0, tiled=True).astype(FULL)


def local(gradients, queries, landmarks, whitening):
    held = 2 * (gradients.size + queries.size + landmarks.size + whitening.size)
    here = lax.axis_size("layer") == LAYERS and lax.axis_size("land") == LANDS
    even = (
        gradients.shape[1] % (128 * PARTS) == 0
        and landmarks.shape[0] % 256 == 0
        and gradients.shape[0] % LAYERS == 0
        and queries.shape[0] == 8 * LANDS
    )
    if here and even and held <= (24 << 20):
        return fused(gradients, queries, landmarks, whitening)
    return staged(gradients, queries, landmarks, whitening)


def solution(mesh):
    return jax.shard_map(
        local,
        mesh=mesh,
        in_specs=(
            P(None, ("layer", "land")),
            P(None, ("layer", "land")),
            P(None, ("layer", "land")),
            P(None, "land"),
        ),
        out_specs=P("land", "layer"),
        check_vma=False,
    )
```

```python
import functools
import jax
import jax.numpy as jnp
from jax import lax
from jax.experimental import pallas as pl
from jax.experimental.pallas import tpu as pltpu
from jax.sharding import PartitionSpec as P

NN = (((1,), (0,)), ((), ()))
NT = (((1,), (1,)), ((), ()))
HALF = jnp.bfloat16
FULL = jnp.float32
LAYERS = 8
LANDS = 4
HUBS = 4
SPREAD = (7, 6, 1, 0, 3, 2, 5, 4)
PARTS = 8
EARLY = 2
STEPS = 2
AHEAD = 1
VMEM_LIMIT = 55136 << 10


def dot(a, b, dims):
    return lax.dot_general(a, b, dims, preferred_element_type=FULL)


def hub(g):
    return (LAYERS + HUBS) // 2 - 1 - g


def kernel(
    factor,
    g_hbm, q_hbm, l_hbm, w_hbm, out_ref,
    g_buf, p_buf, q_buf, l_buf, w_buf, load_sem,
    qs, ps, qr, bs, br, fs, ss, sr,
    sum_send, sum_recv, all_send, all_recv, score_send, score_recv, pair_send, pair_recv,
    hand_send, hand_recv, p_send, p_recv,
):
    n_layer, n_land, n_hub, n_side = LAYERS, LANDS, HUBS, LANDS // 2
    layer = lax.axis_index("layer")
    land = lax.axis_index("land")
    core = lax.rem(land, 2)
    side = lax.div(land, 2)
    own = hub(layer)
    on_one = core == 1
    hub_chip = jnp.logical_and(own >= 0, own < n_hub)
    is_hub = jnp.logical_and(hub_chip, on_one)
    gives_w = jnp.logical_and(hub_chip, core == 0)
    parts = load_sem.shape[0] - 3
    span = l_buf.shape[1] // parts

    loads = [pltpu.make_async_copy(q_hbm, q_buf, load_sem.at[0])]
    for b in range(parts):
        cut = pl.ds(b * span, span)
        loads.append(pltpu.make_async_copy(
            l_hbm.at[:, cut], l_buf.at[:, cut], load_sem.at[1 + b]))
    load_g = pltpu.make_async_copy(g_hbm, g_buf, load_sem.at[1 + parts])
    load_w = pltpu.make_async_copy(w_hbm, w_buf.at[1], load_sem.at[2 + parts])
    for load in loads:
        load.start()

    def device(to_layer, to_land):
        return dict(device_id=(to_layer, to_land), device_id_type=pl.DeviceIdType.MESH)

    def remote(source, target, send, recv, to_layer, to_land):
        return pltpu.make_async_remote_copy(
            src_ref=source, dst_ref=target, send_sem=send, recv_sem=recv,
            **device(to_layer, to_land))

    def elsewhere(k, b):
        return jnp.logical_or(layer != k, land != b)

    barrier = pltpu.get_barrier_semaphore()

    @pl.when(is_hub)
    def _():
        for k in range(n_layer):
            for y in range(n_side):
                @pl.when(elsewhere(k, 2 * y + 1))
                def _():
                    pl.semaphore_signal(barrier, inc=1, **device(k, 2 * y + 1))

    @pl.when(on_one)
    def _():
        pl.semaphore_signal(barrier, inc=1, **device(layer, 2 * side))

    rows = qs.shape[1]
    loads[0].wait()
    part = jnp.zeros((q_buf.shape[0], l_buf.shape[0]), FULL)
    for b in range(parts):
        loads[1 + b].wait()
        if b == parts - AHEAD:
            load_g.start()
        cut = slice(b * span, (b + 1) * span)
        part += dot(q_buf[:, cut], l_buf[:, cut], NT)

    pair = remote(qs, ps, pair_send.at[0], pair_recv.at[0], layer, 2 * side + 1)
    share_w = remote(w_hbm, w_buf.at[0], pair_send.at[1], pair_recv.at[1], layer, 2 * side + 1)

    def sums(g, y):
        return remote(qs.at[g], qr.at[layer, side], sum_send.at[g, y],
                      sum_recv.at[layer, side], hub(g), 2 * y + 1)

    def for_sums(act):
        for g in range(n_hub):
            for y in range(n_side):
                @pl.when(elsewhere(hub(g), 2 * y + 1))
                def _():
                    act(sums(g, y))

    @pl.when(core == 0)
    def _():
        for g in range(n_hub):
            qs[g] = part[g * rows:(g + 1) * rows].astype(HALF)
        pl.semaphore_wait(barrier, 1)
        pair.start()

    pl.when(gives_w)(share_w.start)
    pl.when(is_hub)(load_w.start)

    @pl.when(on_one)
    def _():
        pair.wait_recv()
        for g in range(n_hub):
            both = part[g * rows:(g + 1) * rows] + ps[g].astype(FULL)
            qs[g] = both.astype(HALF)
        pl.semaphore_wait(barrier, n_hub * n_side - is_hub.astype(jnp.int32))
        for_sums(lambda copy: copy.start())

    @pl.when(is_hub)
    def _():
        qr[layer, side] = qs[own]

    count, each = ss.shape[0], ss.shape[3]
    width = p_buf.shape[1] // STEPS

    def share_p(b):
        cut = pl.ds(b * width, width)
        return remote(p_buf.at[0, cut], p_buf.at[1, cut], p_send.at[b], p_recv.at[b],
                      layer, 2 * side + 1 - core)

    def project(step):
        given, b = step < STEPS, step % STEPS
        cut = slice(b * width, (b + 1) * width)
        part = dot(l_buf[cut, :], g_buf[core if given else 1 - core], NT)
        p_buf[0 if given else 2, cut] = part.astype(HALF)
        if given:
            share_p(b).start()

    load_g.wait()
    for b in range(EARLY):
        project(b)

    def gathers(k, y):
        return remote(bs, br.at[own, side], all_send.at[k, y],
                      all_recv.at[own, side], k, 2 * y + 1)

    def for_gathers(act):
        for k in SPREAD:
            for y in range(n_side):
                @pl.when(elsewhere(k, 2 * y + 1))
                def _():
                    act(gathers(k, y))

    @pl.when(is_hub)
    def _():
        total = jnp.zeros(bs.shape, FULL)
        for k in range(n_layer):
            for y in range(n_side):
                @pl.when(elsewhere(k, 2 * y + 1))
                def _():
                    pltpu.make_async_copy(
                        qs.at[0], qr.at[k, y], sum_recv.at[k, y]).wait()
                total += qr[k, y].astype(FULL)
        load_w.wait()
        share_w.wait_recv()

        mixed = total.astype(HALF)
        back = jnp.zeros(bs.shape, FULL)
        for c in range(2):
            white = dot(mixed, w_buf[c], NN).astype(HALF)
            back += dot(white, w_buf[c], NT)
        bs[...] = back.astype(HALF)
        for_gathers(lambda copy: copy.start())
        br[own, side] = bs[...]

    for b in range(EARLY, 2 * STEPS):
        project(b)

    pl.when(gives_w)(share_w.wait_send)
    pl.when(core == 0)(pair.wait_send)
    share = out_ref.shape[0]

    base = count * (1 - core)

    def scores(k, b):
        return remote(ss.at[k, b], sr.at[layer, side], score_send.at[k, b],
                      score_recv.at[layer, side], base + k, b)

    def for_scores(k, bs_, act):
        for b in bs_:
            @pl.when(elsewhere(base + k, b))
            def _():
                act(scores(k, b))

    def hand(h):
        return remote(fs.at[h], fs.at[h], hand_send.at[h], hand_recv.at[h], layer, 2 * side)

    def score(folded, to):
        block = dot(folded, p_buf[1, :, :to], NN) + dot(folded, p_buf[2, :, :to], NN)
        return (block * factor).astype(HALF)

    def put(folded, first, skip=0):
        block = score(folded, count * each)
        lands = range(first, first + folded.shape[0] // share)
        for k in range(count):
            for b in lands:
                if k or b >= skip:
                    row = (b - first) * share
                    ss[k, b] = block[row:row + share, k * each:(k + 1) * each]
        for k in range(count):
            for_scores(k, [b for b in lands if k or b >= skip], lambda copy: copy.start())

    def gather(g):
        row = 0
        for y in range(n_side):
            @pl.when(elsewhere(hub(g), 2 * y + 1))
            def _():
                pltpu.make_async_copy(bs, br.at[g, y], all_recv.at[g, y]).wait()
            row += br[g, y].astype(FULL)
        return row

    for b in range(STEPS):
        share_p(b).wait_recv()

    half = n_hub // 2

    @pl.when(on_one)
    def _():
        for h in range(2):
            top = gather(h * half)
            if h == 0:
                ss[0, 0] = score(top.astype(HALF), each)
                for_scores(0, range(1), lambda copy: copy.start())
            low = gather(h * half + 1)
            fs[h] = jnp.concatenate([top, low], axis=0).astype(HALF)
            hand(h).start()
            put(fs[h], half * h, 1 - h)

    @pl.when(core == 0)
    def _():
        for h in range(2):
            hand(h).wait_recv()
        put(jnp.concatenate([fs[0], fs[1]], axis=0), 0)

    near = 1 - lax.div(layer, count)

    @pl.when(core == near)
    def _():
        sr[layer, side] = ss[lax.rem(layer, count), land]

    @pl.when(on_one)
    def _():
        for_sums(lambda copy: copy.wait_send())
        for h in range(2):
            hand(h).wait_send()

    @pl.when(is_hub)
    def _():
        for_gathers(lambda copy: copy.wait_send())

    for b in range(STEPS):
        share_p(b).wait_send()

    result = jnp.zeros(out_ref.shape, FULL)
    for k in range(n_layer):
        for y in range(n_side):
            @pl.when(elsewhere(k, 2 * y + near))
            def _():
                pltpu.make_async_copy(
                    ss.at[0, 0], sr.at[k, y], score_recv.at[k, y]).wait()
            result += sr[k, y].astype(FULL)
    out_ref[...] = result
    for k in range(count):
        for_scores(k, range(n_land), lambda copy: copy.wait_send())


def fused(gradients, queries, landmarks, whitening):
    n_layer, n_land, n_hub = LAYERS, LANDS, HUBS
    n_rows, width = gradients.shape
    n_query = queries.shape[0]
    n_mark = landmarks.shape[0]
    parts = PARTS
    each, rows, share = n_rows // n_layer, n_query // n_hub, n_query // n_land
    any_space = pl.BlockSpec(memory_space=pltpu.HBM)
    return pl.pallas_call(
        functools.partial(kernel, n_mark ** (-0.5)),
        out_shape=jax.ShapeDtypeStruct((share, each), FULL),
        in_specs=[any_space] * 4,
        out_specs=pl.BlockSpec(memory_space=pltpu.VMEM),
        scratch_shapes=[
            pltpu.VMEM((2, n_rows // 2, width), HALF),
            pltpu.VMEM((3, n_mark, n_rows // 2), HALF),
            pltpu.VMEM((n_query, width), HALF),
            pltpu.VMEM((n_mark, width), HALF),
            pltpu.VMEM((2, *whitening.shape), HALF),
            pltpu.SemaphoreType.DMA((parts + 3,)),
            pltpu.VMEM((n_hub, rows, n_mark), HALF),
            pltpu.VMEM((n_hub, rows, n_mark), HALF),
            pltpu.VMEM((n_layer, n_land // 2, rows, n_mark), HALF),
            pltpu.VMEM((rows, n_mark), HALF),
            pltpu.VMEM((n_hub, n_land // 2, rows, n_mark), HALF),
            pltpu.VMEM((2, n_query // 2, n_mark), HALF),
            pltpu.VMEM((n_layer // 2, n_land, share, each), HALF),
            pltpu.VMEM((n_layer, n_land // 2, share, each), HALF),
            pltpu.SemaphoreType.DMA((n_hub, n_land // 2)),
            pltpu.SemaphoreType.DMA((n_layer, n_land // 2)),
            pltpu.SemaphoreType.DMA((n_layer, n_land // 2)),
            pltpu.SemaphoreType.DMA((n_hub, n_land // 2)),
            pltpu.SemaphoreType.DMA((n_layer // 2, n_land)),
            pltpu.SemaphoreType.DMA((n_layer, n_land // 2)),
            pltpu.SemaphoreType.DMA((2,)),
            pltpu.SemaphoreType.DMA((2,)),
            pltpu.SemaphoreType.DMA((2,)),
            pltpu.SemaphoreType.DMA((2,)),
            pltpu.SemaphoreType.DMA((STEPS,)),
            pltpu.SemaphoreType.DMA((STEPS,)),
        ],
        compiler_params=pltpu.CompilerParams(
            collective_id=0, has_side_effects=True, vmem_limit_bytes=VMEM_LIMIT
        ),
    )(gradients.reshape(2, n_rows // 2, width), queries, landmarks, whitening)


def staged(gradients, queries, landmarks, whitening):
    factor = landmarks.shape[0] ** (-0.5)
    partial = dot(queries, landmarks, NT).astype(HALF)
    query_proj = lax.psum(partial, ("layer", "land"))
    query_white = dot(query_proj, whitening, NN).astype(HALF)
    back = lax.psum(dot(query_white, whitening, NT).astype(HALF), "land")
    spread = dot(back, landmarks, NN).astype(HALF)
    scores = dot(spread, gradients, NT) * factor
    share = lax.psum_scatter(
        scores.astype(HALF), "layer", scatter_dimension=1, tiled=True
    )
    return lax.psum_scatter(share, "land", scatter_dimension=0, tiled=True).astype(FULL)


def local(gradients, queries, landmarks, whitening):
    held = 2 * (gradients.size + queries.size + landmarks.size + whitening.size)
    here = lax.axis_size("layer") == LAYERS and lax.axis_size("land") == LANDS
    even = (
        gradients.shape[1] % (128 * PARTS) == 0
        and landmarks.shape[0] % 256 == 0
        and gradients.shape[0] % LAYERS == 0
        and queries.shape[0] == 8 * LANDS
    )
    if here and even and held <= (24 << 20):
        return fused(gradients, queries, landmarks, whitening)
    return staged(gradients, queries, landmarks, whitening)


def solution(mesh):
    return jax.shard_map(
        local,
        mesh=mesh,
        in_specs=(
            P(None, ("layer", "land")),
            P(None, ("layer", "land")),
            P(None, ("layer", "land")),
            P(None, "land"),
        ),
        out_specs=P("land", "layer"),
        check_vma=False,
    )
```

```python
import functools
import jax
import jax.numpy as jnp
from jax import lax
from jax.experimental import pallas as pl
from jax.experimental.pallas import tpu as pltpu
from jax.sharding import PartitionSpec as P

NN = (((1,), (0,)), ((), ()))
NT = (((1,), (1,)), ((), ()))
HALF = jnp.bfloat16
FULL = jnp.float32
LAYERS = 8
LANDS = 4
HUBS = 4
SPREAD = (7, 6, 1, 0, 3, 2, 5, 4)
PARTS = 8
EARLY = 2
STEPS = 2
AHEAD = 1
VMEM_LIMIT = 55136 << 10


def dot(a, b, dims):
    return lax.dot_general(a, b, dims, preferred_element_type=FULL)


def hub(g):
    return (LAYERS + HUBS) // 2 - 1 - g


def kernel(
    factor,
    g_hbm, q_hbm, l_hbm, w_hbm, out_ref,
    g_buf, p_buf, q_buf, l_buf, w_buf, load_sem,
    qs, ps, qr, bs, br, fs, ss, sr,
    sum_send, sum_recv, all_send, all_recv, score_send, score_recv, pair_send, pair_recv,
    hand_send, hand_recv, p_send, p_recv,
):
    n_layer, n_land, n_hub, n_side = LAYERS, LANDS, HUBS, LANDS // 2
    layer = lax.axis_index("layer")
    land = lax.axis_index("land")
    core = lax.rem(land, 2)
    side = lax.div(land, 2)
    own = hub(layer)
    on_one = core == 1
    hub_chip = jnp.logical_and(own >= 0, own < n_hub)
    is_hub = jnp.logical_and(hub_chip, on_one)
    gives_w = jnp.logical_and(hub_chip, core == 0)
    parts = load_sem.shape[0] - 3
    span = l_buf.shape[1] // parts

    loads = [pltpu.make_async_copy(q_hbm, q_buf, load_sem.at[0])]
    for b in range(parts):
        cut = pl.ds(b * span, span)
        loads.append(pltpu.make_async_copy(
            l_hbm.at[:, cut], l_buf.at[:, cut], load_sem.at[1 + b]))
    load_g = pltpu.make_async_copy(g_hbm, g_buf, load_sem.at[1 + parts])
    load_w = pltpu.make_async_copy(w_hbm, w_buf.at[1], load_sem.at[2 + parts])
    for load in loads:
        load.start()

    def device(to_layer, to_land):
        return dict(device_id=(to_layer, to_land), device_id_type=pl.DeviceIdType.MESH)

    def remote(source, target, send, recv, to_layer, to_land):
        return pltpu.make_async_remote_copy(
            src_ref=source, dst_ref=target, send_sem=send, recv_sem=recv,
            **device(to_layer, to_land))

    def elsewhere(k, b):
        return jnp.logical_or(layer != k, land != b)

    barrier = pltpu.get_barrier_semaphore()

    @pl.when(is_hub)
    def _():
        for k in range(n_layer):
            for y in range(n_side):
                @pl.when(elsewhere(k, 2 * y + 1))
                def _():
                    pl.semaphore_signal(barrier, inc=1, **device(k, 2 * y + 1))

    @pl.when(on_one)
    def _():
        pl.semaphore_signal(barrier, inc=1, **device(layer, 2 * side))

    rows = qs.shape[1]
    loads[0].wait()
    part = jnp.zeros((q_buf.shape[0], l_buf.shape[0]), FULL)
    for b in range(parts):
        loads[1 + b].wait()
        if b == parts - AHEAD:
            load_g.start()
        cut = slice(b * span, (b + 1) * span)
        part += dot(q_buf[:, cut], l_buf[:, cut], NT)

    def pair(g):
        return remote(qs.at[g], ps.at[g], pair_send.at[g], pair_recv.at[g],
                      layer, 2 * side + 1)

    share_w = remote(w_hbm, w_buf.at[0], pair_send.at[n_hub], pair_recv.at[n_hub],
                     layer, 2 * side + 1)

    def sums(g, y):
        return remote(qs.at[g], qr.at[layer, side], sum_send.at[g, y],
                      sum_recv.at[layer, side], hub(g), 2 * y + 1)

    def for_sums(g, act):
        for y in range(n_side):
            @pl.when(elsewhere(hub(g), 2 * y + 1))
            def _():
                act(sums(g, y))

    @pl.when(core == 0)
    def _():
        pl.semaphore_wait(barrier, 1)
        for g in range(n_hub):
            qs[g] = part[g * rows:(g + 1) * rows].astype(HALF)
            pair(g).start()

    pl.when(gives_w)(share_w.start)
    pl.when(is_hub)(load_w.start)

    @pl.when(on_one)
    def _():
        pl.semaphore_wait(barrier, n_hub * n_side - is_hub.astype(jnp.int32))
        for g in range(n_hub):
            pair(g).wait_recv()
            both = part[g * rows:(g + 1) * rows] + ps[g].astype(FULL)
            qs[g] = both.astype(HALF)
            for_sums(g, lambda copy: copy.start())

    @pl.when(is_hub)
    def _():
        qr[layer, side] = qs[own]

    count, each = ss.shape[0], ss.shape[3]
    width = p_buf.shape[1] // STEPS

    def share_p(b):
        cut = pl.ds(b * width, width)
        return remote(p_buf.at[0, cut], p_buf.at[1, cut], p_send.at[b], p_recv.at[b],
                      layer, 2 * side + 1 - core)

    def project(b, given):
        cut = pl.ds(pl.multiple_of(b * width, width), width)
        part = dot(l_buf[cut, :], g_buf[core if given else 1 - core], NT)
        p_buf[0 if given else 2, cut] = part.astype(HALF)
        if given:
            share_p(b).start()

    load_g.wait()
    def loop(low, high, given):
        def step(b, carry):
            project(b, given)
            return carry

        lax.fori_loop(low, high, step, 0)

    loop(0, STEPS, True)
    early = (lax.div(layer, 2) == 1).astype(jnp.int32)
    loop(0, early, False)

    def gathers(k, y):
        return remote(bs, br.at[own, side], all_send.at[k, y],
                      all_recv.at[own, side], k, 2 * y + 1)

    def for_gathers(act):
        for k in SPREAD:
            for y in range(n_side):
                @pl.when(elsewhere(k, 2 * y + 1))
                def _():
                    act(gathers(k, y))

    @pl.when(is_hub)
    def _():
        total = jnp.zeros(bs.shape, FULL)
        for k in range(n_layer):
            for y in range(n_side):
                @pl.when(elsewhere(k, 2 * y + 1))
                def _():
                    pltpu.make_async_copy(
                        qs.at[0], qr.at[k, y], sum_recv.at[k, y]).wait()
                total += qr[k, y].astype(FULL)
        load_w.wait()
        share_w.wait_recv()

        mixed = total.astype(HALF)
        back = jnp.zeros(bs.shape, FULL)
        for c in range(2):
            white = dot(mixed, w_buf[c], NN).astype(HALF)
            back += dot(white, w_buf[c], NT)
        bs[...] = back.astype(HALF)
        for_gathers(lambda copy: copy.start())
        br[own, side] = bs[...]

    loop(early, STEPS, False)

    pl.when(gives_w)(share_w.wait_send)

    @pl.when(core == 0)
    def _():
        for g in range(n_hub):
            pair(g).wait_send()

    share = out_ref.shape[0]

    base = count * (1 - core)

    def scores(k, b):
        return remote(ss.at[k, b], sr.at[layer, side], score_send.at[k, b],
                      score_recv.at[layer, side], base + k, b)

    def for_scores(k, bs_, act):
        for b in bs_:
            @pl.when(elsewhere(base + k, b))
            def _():
                act(scores(k, b))

    def hand(h):
        return remote(fs.at[h], fs.at[h], hand_send.at[h], hand_recv.at[h], layer, 2 * side)

    def score(folded, to):
        block = dot(folded, p_buf[1, :, :to], NN) + dot(folded, p_buf[2, :, :to], NN)
        return (block * factor).astype(HALF)

    def put(folded, first, skip=0):
        block = score(folded, count * each)
        lands = range(first, first + folded.shape[0] // share)
        for k in range(count):
            for b in lands:
                if k or b >= skip:
                    row = (b - first) * share
                    ss[k, b] = block[row:row + share, k * each:(k + 1) * each]
            for_scores(k, [b for b in lands if k or b >= skip], lambda copy: copy.start())

    def gather(g):
        row = 0
        for y in range(n_side):
            @pl.when(elsewhere(hub(g), 2 * y + 1))
            def _():
                pltpu.make_async_copy(bs, br.at[g, y], all_recv.at[g, y]).wait()
            row += br[g, y].astype(FULL)
        return row

    for b in range(STEPS):
        share_p(b).wait_recv()

    half = n_hub // 2

    @pl.when(on_one)
    def _():
        for h in range(2):
            top = gather(h * half)
            if h == 0:
                ss[0, 0] = score(top.astype(HALF), each)
                for_scores(0, range(1), lambda copy: copy.start())
            low = gather(h * half + 1)
            fs[h] = jnp.concatenate([top, low], axis=0).astype(HALF)
            hand(h).start()
            put(fs[h], half * h, 1 - h)

    @pl.when(core == 0)
    def _():
        for h in range(2):
            hand(h).wait_recv()
            put(fs[h], half * h)

    near = 1 - lax.div(layer, count)

    @pl.when(core == near)
    def _():
        sr[layer, side] = ss[lax.rem(layer, count), land]

    @pl.when(on_one)
    def _():
        for g in range(n_hub):
            for_sums(g, lambda copy: copy.wait_send())
        for h in range(2):
            hand(h).wait_send()

    @pl.when(is_hub)
    def _():
        for_gathers(lambda copy: copy.wait_send())

    for b in range(STEPS):
        share_p(b).wait_send()

    for k in range(count):
        for_scores(k, range(n_land), lambda copy: copy.wait_send())

    result = jnp.zeros(out_ref.shape, FULL)
    for k in range(n_layer):
        for y in range(n_side):
            @pl.when(elsewhere(k, 2 * y + near))
            def _():
                pltpu.make_async_copy(
                    ss.at[0, 0], sr.at[k, y], score_recv.at[k, y]).wait()
            result += sr[k, y].astype(FULL)
    out_ref[...] = result


def fused(gradients, queries, landmarks, whitening):
    n_layer, n_land, n_hub = LAYERS, LANDS, HUBS
    n_rows, width = gradients.shape
    n_query = queries.shape[0]
    n_mark = landmarks.shape[0]
    parts = PARTS
    each, rows, share = n_rows // n_layer, n_query // n_hub, n_query // n_land
    any_space = pl.BlockSpec(memory_space=pltpu.HBM)
    return pl.pallas_call(
        functools.partial(kernel, n_mark ** (-0.5)),
        out_shape=jax.ShapeDtypeStruct((share, each), FULL),
        in_specs=[any_space] * 4,
        out_specs=pl.BlockSpec(memory_space=pltpu.VMEM),
        scratch_shapes=[
            pltpu.VMEM((2, n_rows // 2, width), HALF),
            pltpu.VMEM((3, n_mark, n_rows // 2), HALF),
            pltpu.VMEM((n_query, width), HALF),
            pltpu.VMEM((n_mark, width), HALF),
            pltpu.VMEM((2, *whitening.shape), HALF),
            pltpu.SemaphoreType.DMA((parts + 3,)),
            pltpu.VMEM((n_hub, rows, n_mark), HALF),
            pltpu.VMEM((n_hub, rows, n_mark), HALF),
            pltpu.VMEM((n_layer, n_land // 2, rows, n_mark), HALF),
            pltpu.VMEM((rows, n_mark), HALF),
            pltpu.VMEM((n_hub, n_land // 2, rows, n_mark), HALF),
            pltpu.VMEM((2, n_query // 2, n_mark), HALF),
            pltpu.VMEM((n_layer // 2, n_land, share, each), HALF),
            pltpu.VMEM((n_layer, n_land // 2, share, each), HALF),
            pltpu.SemaphoreType.DMA((n_hub, n_land // 2)),
            pltpu.SemaphoreType.DMA((n_layer, n_land // 2)),
            pltpu.SemaphoreType.DMA((n_layer, n_land // 2)),
            pltpu.SemaphoreType.DMA((n_hub, n_land // 2)),
            pltpu.SemaphoreType.DMA((n_layer // 2, n_land)),
            pltpu.SemaphoreType.DMA((n_layer, n_land // 2)),
            pltpu.SemaphoreType.DMA((n_hub + 1,)),
            pltpu.SemaphoreType.DMA((n_hub + 1,)),
            pltpu.SemaphoreType.DMA((2,)),
            pltpu.SemaphoreType.DMA((2,)),
            pltpu.SemaphoreType.DMA((STEPS,)),
            pltpu.SemaphoreType.DMA((STEPS,)),
        ],
        compiler_params=pltpu.CompilerParams(
            collective_id=0, has_side_effects=True, vmem_limit_bytes=VMEM_LIMIT
        ),
    )(gradients.reshape(2, n_rows // 2, width), queries, landmarks, whitening)


def staged(gradients, queries, landmarks, whitening):
    factor = landmarks.shape[0] ** (-0.5)
    partial = dot(queries, landmarks, NT).astype(HALF)
    query_proj = lax.psum(partial, ("layer", "land"))
    query_white = dot(query_proj, whitening, NN).astype(HALF)
    back = lax.psum(dot(query_white, whitening, NT).astype(HALF), "land")
    spread = dot(back, landmarks, NN).astype(HALF)
    scores = dot(spread, gradients, NT) * factor
    share = lax.psum_scatter(
        scores.astype(HALF), "layer", scatter_dimension=1, tiled=True
    )
    return lax.psum_scatter(share, "land", scatter_dimension=0, tiled=True).astype(FULL)


def local(gradients, queries, landmarks, whitening):
    held = 2 * (gradients.size + queries.size + landmarks.size + whitening.size)
    here = lax.axis_size("layer") == LAYERS and lax.axis_size("land") == LANDS
    even = (
        gradients.shape[1] % (128 * PARTS) == 0
        and landmarks.shape[0] % 256 == 0
        and gradients.shape[0] % LAYERS == 0
        and queries.shape[0] == 8 * LANDS
    )
    if here and even and held <= (24 << 20):
        return fused(gradients, queries, landmarks, whitening)
    return staged(gradients, queries, landmarks, whitening)


def solution(mesh):
    return jax.shard_map(
        local,
        mesh=mesh,
        in_specs=(
            P(None, ("layer", "land")),
            P(None, ("layer", "land")),
            P(None, ("layer", "land")),
            P(None, "land"),
        ),
        out_specs=P("land", "layer"),
        check_vma=False,
    )
```

```python
import functools
import jax
import jax.numpy as jnp
from jax import lax
from jax.experimental import pallas as pl
from jax.experimental.pallas import tpu as pltpu
from jax.sharding import PartitionSpec as P

NN = (((1,), (0,)), ((), ()))
NT = (((1,), (1,)), ((), ()))
HALF = jnp.bfloat16
FULL = jnp.float32
LAYERS = 8
LANDS = 4
HUBS = 4
SPREAD = (7, 6, 1, 0, 3, 2, 5, 4)
PARTS = 8
EARLY = 2
STEPS = 2
AHEAD = 1
VMEM_LIMIT = 55136 << 10


def dot(a, b, dims):
    return lax.dot_general(a, b, dims, preferred_element_type=FULL)


def hub(g):
    return (LAYERS + HUBS) // 2 - 1 - g


def kernel(
    factor,
    g_hbm, q_hbm, l_hbm, w_hbm, out_ref,
    g_buf, p_buf, q_buf, l_buf, w_buf, load_sem,
    qs, ps, qr, bs, br, fs, ss, sr,
    sum_send, sum_recv, all_send, all_recv, score_send, score_recv, pair_send, pair_recv,
    hand_send, hand_recv, p_send, p_recv,
):
    n_layer, n_land, n_hub, n_side = LAYERS, LANDS, HUBS, LANDS // 2
    layer = lax.axis_index("layer")
    land = lax.axis_index("land")
    core = lax.rem(land, 2)
    side = lax.div(land, 2)
    own = hub(layer)
    on_one = core == 1
    hub_chip = jnp.logical_and(own >= 0, own < n_hub)
    is_hub = jnp.logical_and(hub_chip, on_one)
    gives_w = jnp.logical_and(hub_chip, core == 0)
    parts = load_sem.shape[0] - 3
    span = l_buf.shape[1] // parts

    loads = [pltpu.make_async_copy(q_hbm, q_buf, load_sem.at[0])]
    for b in range(parts):
        cut = pl.ds(b * span, span)
        loads.append(pltpu.make_async_copy(
            l_hbm.at[:, cut], l_buf.at[:, cut], load_sem.at[1 + b]))
    load_g = pltpu.make_async_copy(g_hbm, g_buf, load_sem.at[1 + parts])
    load_w = pltpu.make_async_copy(w_hbm, w_buf.at[1], load_sem.at[2 + parts])
    for load in loads:
        load.start()

    def device(to_layer, to_land):
        return dict(device_id=(to_layer, to_land), device_id_type=pl.DeviceIdType.MESH)

    def remote(source, target, send, recv, to_layer, to_land):
        return pltpu.make_async_remote_copy(
            src_ref=source, dst_ref=target, send_sem=send, recv_sem=recv,
            **device(to_layer, to_land))

    def elsewhere(k, b):
        return jnp.logical_or(layer != k, land != b)

    barrier = pltpu.get_barrier_semaphore()

    @pl.when(is_hub)
    def _():
        for k in range(n_layer):
            for y in range(n_side):
                @pl.when(elsewhere(k, 2 * y + 1))
                def _():
                    pl.semaphore_signal(barrier, inc=1, **device(k, 2 * y + 1))

    @pl.when(on_one)
    def _():
        pl.semaphore_signal(barrier, inc=1, **device(layer, 2 * side))

    rows = qs.shape[1]
    loads[0].wait()
    part = jnp.zeros((q_buf.shape[0], l_buf.shape[0]), FULL)
    for b in range(parts):
        loads[1 + b].wait()
        if b == parts - AHEAD:
            load_g.start()
        cut = slice(b * span, (b + 1) * span)
        part += dot(q_buf[:, cut], l_buf[:, cut], NT)

    def pair(g):
        return remote(qs.at[g], ps.at[g], pair_send.at[g], pair_recv.at[g],
                      layer, 2 * side + 1)

    share_w = remote(w_hbm, w_buf.at[0], pair_send.at[n_hub], pair_recv.at[n_hub],
                     layer, 2 * side + 1)

    def sums(g, y):
        return remote(qs.at[g], qr.at[layer, side], sum_send.at[g, y],
                      sum_recv.at[layer, side], hub(g), 2 * y + 1)

    def for_sums(g, act):
        for y in range(n_side):
            @pl.when(elsewhere(hub(g), 2 * y + 1))
            def _():
                act(sums(g, y))

    @pl.when(core == 0)
    def _():
        pl.semaphore_wait(barrier, 1)
        for g in range(n_hub):
            qs[g] = part[g * rows:(g + 1) * rows].astype(HALF)
            pair(g).start()

    pl.when(gives_w)(share_w.start)
    pl.when(is_hub)(load_w.start)

    @pl.when(on_one)
    def _():
        pl.semaphore_wait(barrier, n_hub * n_side - is_hub.astype(jnp.int32))
        for g in range(n_hub):
            pair(g).wait_recv()
            both = part[g * rows:(g + 1) * rows] + ps[g].astype(FULL)
            qs[g] = both.astype(HALF)
            for_sums(g, lambda copy: copy.start())

    @pl.when(is_hub)
    def _():
        qr[layer, side] = qs[own]

    count, each = ss.shape[0], ss.shape[3]
    width = p_buf.shape[1] // STEPS

    def share_p(b):
        cut = pl.ds(b * width, width)
        return remote(p_buf.at[0, cut], p_buf.at[1, cut], p_send.at[b], p_recv.at[b],
                      layer, 2 * side + 1 - core)

    def project(b, given):
        cut = pl.ds(pl.multiple_of(b * width, width), width)
        part = dot(l_buf[cut, :], g_buf[core if given else 1 - core], NT)
        p_buf[0 if given else 2, cut] = part.astype(HALF)
        if given:
            share_p(b).start()

    load_g.wait()
    def loop(low, high, given):
        def step(b, carry):
            project(b, given)
            return carry

        lax.fori_loop(low, high, step, 0)

    loop(0, STEPS, True)
    early = (lax.div(layer, 2) == 1).astype(jnp.int32)
    loop(0, early, False)

    def gathers(k, y):
        return remote(bs, br.at[own, side], all_send.at[k, y],
                      all_recv.at[own, side], k, 2 * y + 1)

    def for_gathers(act):
        for k in SPREAD:
            for y in range(n_side):
                @pl.when(elsewhere(k, 2 * y + 1))
                def _():
                    act(gathers(k, y))

    @pl.when(is_hub)
    def _():
        total = jnp.zeros(bs.shape, FULL)
        for k in range(n_layer):
            for y in range(n_side):
                @pl.when(elsewhere(k, 2 * y + 1))
                def _():
                    pltpu.make_async_copy(
                        qs.at[0], qr.at[k, y], sum_recv.at[k, y]).wait()
                total += qr[k, y].astype(FULL)
        load_w.wait()
        share_w.wait_recv()

        mixed = total.astype(HALF)
        back = jnp.zeros(bs.shape, FULL)
        for c in range(2):
            white = dot(mixed, w_buf[c], NN).astype(HALF)
            back += dot(white, w_buf[c], NT)
        bs[...] = back.astype(HALF)
        for_gathers(lambda copy: copy.start())
        br[own, side] = bs[...]

    loop(early, STEPS, False)

    pl.when(gives_w)(share_w.wait_send)

    @pl.when(core == 0)
    def _():
        for g in range(n_hub):
            pair(g).wait_send()

    share = out_ref.shape[0]

    base = count * (1 - core)

    def scores(k, b):
        return remote(ss.at[k, b], sr.at[layer, side], score_send.at[k, b],
                      score_recv.at[layer, side], base + k, b)

    def for_scores(k, bs_, act):
        for b in bs_:
            @pl.when(elsewhere(base + k, b))
            def _():
                act(scores(k, b))

    def hand(h):
        return remote(fs.at[h], fs.at[h], hand_send.at[h], hand_recv.at[h], layer, 2 * side)

    def score(folded, to):
        block = dot(folded, p_buf[1, :, :to], NN) + dot(folded, p_buf[2, :, :to], NN)
        return block * factor

    def put(folded, first, skip=0):
        block = score(folded, count * each)
        lands = range(first, first + folded.shape[0] // share)
        for k in range(count):
            for b in lands:
                if k or b >= skip:
                    row = (b - first) * share
                    ss[k, b] = block[row:row + share, k * each:(k + 1) * each].astype(HALF)
            for_scores(k, [b for b in lands if k or b >= skip], lambda copy: copy.start())

    def gather(g):
        row = 0
        for y in range(n_side):
            @pl.when(elsewhere(hub(g), 2 * y + 1))
            def _():
                pltpu.make_async_copy(bs, br.at[g, y], all_recv.at[g, y]).wait()
            row += br[g, y].astype(FULL)
        return row

    for b in range(STEPS):
        share_p(b).wait_recv()

    half = n_hub // 2

    @pl.when(on_one)
    def _():
        for h in range(2):
            top = gather(h * half)
            if h == 0:
                ss[0, 0] = score(top.astype(HALF), each).astype(HALF)
                for_scores(0, range(1), lambda copy: copy.start())
            low = gather(h * half + 1)
            fs[h] = jnp.concatenate([top, low], axis=0).astype(HALF)
            hand(h).start()
            put(fs[h], half * h, 1 - h)

    @pl.when(core == 0)
    def _():
        for h in range(2):
            hand(h).wait_recv()
            put(fs[h], half * h)

    near = 1 - lax.div(layer, count)

    @pl.when(core == near)
    def _():
        sr[layer, side] = ss[lax.rem(layer, count), land]

    @pl.when(on_one)
    def _():
        for g in range(n_hub):
            for_sums(g, lambda copy: copy.wait_send())
        for h in range(2):
            hand(h).wait_send()

    @pl.when(is_hub)
    def _():
        for_gathers(lambda copy: copy.wait_send())

    for b in range(STEPS):
        share_p(b).wait_send()

    for k in range(count):
        for_scores(k, range(n_land), lambda copy: copy.wait_send())

    result = jnp.zeros(out_ref.shape, FULL)
    for k in range(n_layer):
        for y in range(n_side):
            @pl.when(elsewhere(k, 2 * y + near))
            def _():
                pltpu.make_async_copy(
                    ss.at[0, 0], sr.at[k, y], score_recv.at[k, y]).wait()
            result += sr[k, y].astype(FULL)
    out_ref[...] = result


def fused(gradients, queries, landmarks, whitening):
    n_layer, n_land, n_hub = LAYERS, LANDS, HUBS
    n_rows, width = gradients.shape
    n_query = queries.shape[0]
    n_mark = landmarks.shape[0]
    parts = PARTS
    each, rows, share = n_rows // n_layer, n_query // n_hub, n_query // n_land
    any_space = pl.BlockSpec(memory_space=pltpu.HBM)
    return pl.pallas_call(
        functools.partial(kernel, n_mark ** (-0.5)),
        out_shape=jax.ShapeDtypeStruct((share, each), FULL),
        in_specs=[any_space] * 4,
        out_specs=pl.BlockSpec(memory_space=pltpu.VMEM),
        scratch_shapes=[
            pltpu.VMEM((2, n_rows // 2, width), HALF),
            pltpu.VMEM((3, n_mark, n_rows // 2), HALF),
            pltpu.VMEM((n_query, width), HALF),
            pltpu.VMEM((n_mark, width), HALF),
            pltpu.VMEM((2, *whitening.shape), HALF),
            pltpu.SemaphoreType.DMA((parts + 3,)),
            pltpu.VMEM((n_hub, rows, n_mark), HALF),
            pltpu.VMEM((n_hub, rows, n_mark), HALF),
            pltpu.VMEM((n_layer, n_land // 2, rows, n_mark), HALF),
            pltpu.VMEM((rows, n_mark), HALF),
            pltpu.VMEM((n_hub, n_land // 2, rows, n_mark), HALF),
            pltpu.VMEM((2, n_query // 2, n_mark), HALF),
            pltpu.VMEM((n_layer // 2, n_land, share, each), HALF),
            pltpu.VMEM((n_layer, n_land // 2, share, each), HALF),
            pltpu.SemaphoreType.DMA((n_hub, n_land // 2)),
            pltpu.SemaphoreType.DMA((n_layer, n_land // 2)),
            pltpu.SemaphoreType.DMA((n_layer, n_land // 2)),
            pltpu.SemaphoreType.DMA((n_hub, n_land // 2)),
            pltpu.SemaphoreType.DMA((n_layer // 2, n_land)),
            pltpu.SemaphoreType.DMA((n_layer, n_land // 2)),
            pltpu.SemaphoreType.DMA((n_hub + 1,)),
            pltpu.SemaphoreType.DMA((n_hub + 1,)),
            pltpu.SemaphoreType.DMA((2,)),
            pltpu.SemaphoreType.DMA((2,)),
            pltpu.SemaphoreType.DMA((STEPS,)),
            pltpu.SemaphoreType.DMA((STEPS,)),
        ],
        compiler_params=pltpu.CompilerParams(
            collective_id=0, has_side_effects=True, vmem_limit_bytes=VMEM_LIMIT
        ),
    )(gradients.reshape(2, n_rows // 2, width), queries, landmarks, whitening)


def staged(gradients, queries, landmarks, whitening):
    factor = landmarks.shape[0] ** (-0.5)
    partial = dot(queries, landmarks, NT).astype(HALF)
    query_proj = lax.psum(partial, ("layer", "land"))
    query_white = dot(query_proj, whitening, NN).astype(HALF)
    back = lax.psum(dot(query_white, whitening, NT).astype(HALF), "land")
    spread = dot(back, landmarks, NN).astype(HALF)
    scores = dot(spread, gradients, NT) * factor
    share = lax.psum_scatter(
        scores.astype(HALF), "layer", scatter_dimension=1, tiled=True
    )
    return lax.psum_scatter(share, "land", scatter_dimension=0, tiled=True).astype(FULL)


def local(gradients, queries, landmarks, whitening):
    held = 2 * (gradients.size + queries.size + landmarks.size + whitening.size)
    here = lax.axis_size("layer") == LAYERS and lax.axis_size("land") == LANDS
    even = (
        gradients.shape[1] % (128 * PARTS) == 0
        and landmarks.shape[0] % 256 == 0
        and gradients.shape[0] % LAYERS == 0
        and queries.shape[0] == 8 * LANDS
    )
    if here and even and held <= (24 << 20):
        return fused(gradients, queries, landmarks, whitening)
    return staged(gradients, queries, landmarks, whitening)


def solution(mesh):
    return jax.shard_map(
        local,
        mesh=mesh,
        in_specs=(
            P(None, ("layer", "land")),
            P(None, ("layer", "land")),
            P(None, ("layer", "land")),
            P(None, "land"),
        ),
        out_specs=P("land", "layer"),
        check_vma=False,
    )
```

```python
import functools
import jax
import jax.numpy as jnp
from jax import lax
from jax.experimental import pallas as pl
from jax.experimental.pallas import tpu as pltpu
from jax.sharding import PartitionSpec as P

NN = (((1,), (0,)), ((), ()))
NT = (((1,), (1,)), ((), ()))
HALF = jnp.bfloat16
FULL = jnp.float32
LAYERS = 8
LANDS = 4
HUBS = 4
SPREAD = (7, 6, 1, 0, 3, 2, 5, 4)
PARTS = 8
EARLY = 2
STEPS = 2
AHEAD = 3
VMEM_LIMIT = 55136 << 10


def dot(a, b, dims):
    return lax.dot_general(a, b, dims, preferred_element_type=FULL)


def hub(g):
    return (LAYERS + HUBS) // 2 - 1 - g


def kernel(
    factor,
    g_hbm, q_hbm, l_hbm, w_hbm, out_ref,
    g_buf, p_buf, q_buf, l_buf, w_buf, load_sem,
    qs, ps, qr, bs, br, fs, ss, sr,
    sum_send, sum_recv, all_send, all_recv, score_send, score_recv, pair_send, pair_recv,
    hand_send, hand_recv, p_send, p_recv,
):
    n_layer, n_land, n_hub, n_side = LAYERS, LANDS, HUBS, LANDS // 2
    layer = lax.axis_index("layer")
    land = lax.axis_index("land")
    core = lax.rem(land, 2)
    side = lax.div(land, 2)
    own = hub(layer)
    on_one = core == 1
    hub_chip = jnp.logical_and(own >= 0, own < n_hub)
    is_hub = jnp.logical_and(hub_chip, on_one)
    direct = layer >= n_layer - 2
    direct_zero = jnp.logical_and(direct, core == 0)
    gives_w = jnp.logical_and(hub_chip, core == 0)
    parts = load_sem.shape[0] - 3
    span = l_buf.shape[1] // parts

    loads = [pltpu.make_async_copy(q_hbm, q_buf, load_sem.at[0])]
    for b in range(parts):
        cut = pl.ds(b * span, span)
        loads.append(pltpu.make_async_copy(
            l_hbm.at[:, cut], l_buf.at[:, cut], load_sem.at[1 + b]))
    load_g = pltpu.make_async_copy(g_hbm, g_buf, load_sem.at[1 + parts])
    load_w = pltpu.make_async_copy(w_hbm, w_buf.at[1], load_sem.at[2 + parts])
    for load in loads:
        load.start()

    def device(to_layer, to_land):
        return dict(device_id=(to_layer, to_land), device_id_type=pl.DeviceIdType.MESH)

    def remote(source, target, send, recv, to_layer, to_land):
        return pltpu.make_async_remote_copy(
            src_ref=source, dst_ref=target, send_sem=send, recv_sem=recv,
            **device(to_layer, to_land))

    def elsewhere(k, b):
        return jnp.logical_or(layer != k, land != b)

    barrier = pltpu.get_barrier_semaphore()

    @pl.when(is_hub)
    def _():
        for k in range(n_layer):
            for y in range(n_side):
                @pl.when(elsewhere(k, 2 * y + 1))
                def _():
                    pl.semaphore_signal(barrier, inc=1, **device(k, 2 * y + 1))

                if k >= n_layer - 2:
                    @pl.when(own == 0)
                    def _():
                        pl.semaphore_signal(barrier, inc=1, **device(k, 2 * y))

    @pl.when(on_one)
    def _():
        pl.semaphore_signal(barrier, inc=1, **device(layer, 2 * side))

    rows = qs.shape[1]
    loads[0].wait()
    part = jnp.zeros((q_buf.shape[0], l_buf.shape[0]), FULL)
    for b in range(parts):
        loads[1 + b].wait()
        if b == parts - AHEAD:
            load_g.start()
        cut = slice(b * span, (b + 1) * span)
        part += dot(q_buf[:, cut], l_buf[:, cut], NT)

    def pair(g):
        return remote(qs.at[g], ps.at[g], pair_send.at[g], pair_recv.at[g],
                      layer, 2 * side + 1)

    share_w = remote(w_hbm, w_buf.at[0], pair_send.at[n_hub], pair_recv.at[n_hub],
                     layer, 2 * side + 1)

    def sums(g, y):
        slot = layer + 2 * (1 - core)
        return remote(qs.at[g], qr.at[slot, side], sum_send.at[g, y],
                      sum_recv.at[slot, side], hub(g), 2 * y + 1)

    def for_sums(g, act):
        for y in range(n_side):
            @pl.when(elsewhere(hub(g), 2 * y + 1))
            def _():
                act(sums(g, y))

    @pl.when(core == 0)
    def _():
        pl.semaphore_wait(barrier, 1 + n_side * direct.astype(jnp.int32))
        for g in range(n_hub):
            qs[g] = part[g * rows:(g + 1) * rows].astype(HALF)
            if g:
                pair(g).start()
            else:
                @pl.when(direct)
                def _():
                    for_sums(g, lambda copy: copy.start())

                pl.when(jnp.logical_not(direct))(pair(g).start)

    pl.when(gives_w)(share_w.start)
    pl.when(is_hub)(load_w.start)

    @pl.when(on_one)
    def _():
        pl.semaphore_wait(barrier, n_hub * n_side - is_hub.astype(jnp.int32))
        for g in range(n_hub):
            def add():
                pair(g).wait_recv()
                both = part[g * rows:(g + 1) * rows] + ps[g].astype(FULL)
                qs[g] = both.astype(HALF)

            if g:
                add()
            else:
                @pl.when(direct)
                def _():
                    qs[g] = part[g * rows:(g + 1) * rows].astype(HALF)

                pl.when(jnp.logical_not(direct))(add)
            for_sums(g, lambda copy: copy.start())

    @pl.when(is_hub)
    def _():
        qr[layer, side] = qs[own]

    count, each = ss.shape[0], ss.shape[3]
    width = p_buf.shape[1] // STEPS

    def share_p(b):
        cut = pl.ds(b * width, width)
        return remote(p_buf.at[0, cut], p_buf.at[1, cut], p_send.at[b], p_recv.at[b],
                      layer, 2 * side + 1 - core)

    def project(b, given):
        cut = pl.ds(pl.multiple_of(b * width, width), width)
        part = dot(l_buf[cut, :], g_buf[core if given else 1 - core], NT)
        p_buf[0 if given else 2, cut] = part.astype(HALF)
        if given:
            share_p(b).start()

    load_g.wait()
    def loop(low, high, given):
        def step(b, carry):
            project(b, given)
            return carry

        lax.fori_loop(low, high, step, 0)

    loop(0, STEPS, True)
    early = (lax.div(layer, 2) == 1).astype(jnp.int32)
    loop(0, early, False)

    def gathers(k, y):
        return remote(bs, br.at[own, side], all_send.at[k, y],
                      all_recv.at[own, side], k, 2 * y + 1)

    def for_gathers(act):
        for k in SPREAD:
            for y in range(n_side):
                @pl.when(elsewhere(k, 2 * y + 1))
                def _():
                    act(gathers(k, y))

    @pl.when(is_hub)
    def _():
        @pl.when(own > 0)
        def _():
            qr[n_layer:] = jnp.zeros((2, *qr.shape[1:]), HALF)

        total = jnp.zeros(bs.shape, FULL)
        for k in range(n_layer + 2):
            for y in range(n_side):
                @pl.when(own == 0 if k >= n_layer else elsewhere(k, 2 * y + 1))
                def _():
                    pltpu.make_async_copy(
                        qs.at[0], qr.at[k, y], sum_recv.at[k, y]).wait()
                total += qr[k, y].astype(FULL)
        load_w.wait()
        share_w.wait_recv()

        mixed = total.astype(HALF)
        back = jnp.zeros(bs.shape, FULL)
        for c in range(2):
            white = dot(mixed, w_buf[c], NN).astype(HALF)
            back += dot(white, w_buf[c], NT)
        bs[...] = back.astype(HALF)
        for_gathers(lambda copy: copy.start())
        br[own, side] = bs[...]

    loop(early, STEPS, False)

    pl.when(gives_w)(share_w.wait_send)

    @pl.when(core == 0)
    def _():
        for g in range(1, n_hub):
            pair(g).wait_send()

        @pl.when(direct)
        def _():
            for_sums(0, lambda copy: copy.wait_send())

        pl.when(jnp.logical_not(direct))(pair(0).wait_send)

    share = out_ref.shape[0]

    base = count * (1 - core)

    def scores(k, b):
        return remote(ss.at[k, b], sr.at[layer, side], score_send.at[k, b],
                      score_recv.at[layer, side], base + k, b)

    def for_scores(k, bs_, act):
        for b in bs_:
            @pl.when(elsewhere(base + k, b))
            def _():
                act(scores(k, b))

    def hand(h):
        return remote(fs.at[h], fs.at[h], hand_send.at[h], hand_recv.at[h], layer, 2 * side)

    def score(folded, to):
        block = dot(folded, p_buf[1, :, :to], NN) + dot(folded, p_buf[2, :, :to], NN)
        return block * factor

    def put(folded, first, skip=0):
        block = score(folded, count * each)
        lands = range(first, first + folded.shape[0] // share)
        for k in range(count):
            for b in lands:
                if k or b >= skip:
                    row = (b - first) * share
                    ss[k, b] = block[row:row + share, k * each:(k + 1) * each].astype(HALF)
            for_scores(k, [b for b in lands if k or b >= skip], lambda copy: copy.start())

    def gather(g):
        row = 0
        for y in range(n_side):
            @pl.when(elsewhere(hub(g), 2 * y + 1))
            def _():
                pltpu.make_async_copy(bs, br.at[g, y], all_recv.at[g, y]).wait()
            row += br[g, y].astype(FULL)
        return row

    for b in range(STEPS):
        share_p(b).wait_recv()

    half = n_hub // 2

    @pl.when(on_one)
    def _():
        for h in range(2):
            top = gather(h * half)
            if h == 0:
                ss[0, 0] = score(top.astype(HALF), each).astype(HALF)
                for_scores(0, range(1), lambda copy: copy.start())
            low = gather(h * half + 1)
            fs[h] = jnp.concatenate([top, low], axis=0).astype(HALF)
            hand(h).start()
            put(fs[h], half * h, 1 - h)

    @pl.when(core == 0)
    def _():
        for h in range(2):
            hand(h).wait_recv()
            put(fs[h], half * h)

    near = 1 - lax.div(layer, count)

    @pl.when(core == near)
    def _():
        sr[layer, side] = ss[lax.rem(layer, count), land]

    @pl.when(on_one)
    def _():
        for g in range(n_hub):
            for_sums(g, lambda copy: copy.wait_send())
        for h in range(2):
            hand(h).wait_send()

    @pl.when(is_hub)
    def _():
        for_gathers(lambda copy: copy.wait_send())

    for b in range(STEPS):
        share_p(b).wait_send()

    for k in range(count):
        for_scores(k, range(n_land), lambda copy: copy.wait_send())

    result = jnp.zeros(out_ref.shape, FULL)
    for k in range(n_layer):
        for y in range(n_side):
            @pl.when(elsewhere(k, 2 * y + near))
            def _():
                pltpu.make_async_copy(
                    ss.at[0, 0], sr.at[k, y], score_recv.at[k, y]).wait()
            result += sr[k, y].astype(FULL)
    out_ref[...] = result


def fused(gradients, queries, landmarks, whitening):
    n_layer, n_land, n_hub = LAYERS, LANDS, HUBS
    n_rows, width = gradients.shape
    n_query = queries.shape[0]
    n_mark = landmarks.shape[0]
    parts = PARTS
    each, rows, share = n_rows // n_layer, n_query // n_hub, n_query // n_land
    any_space = pl.BlockSpec(memory_space=pltpu.HBM)
    return pl.pallas_call(
        functools.partial(kernel, n_mark ** (-0.5)),
        out_shape=jax.ShapeDtypeStruct((share, each), FULL),
        in_specs=[any_space] * 4,
        out_specs=pl.BlockSpec(memory_space=pltpu.VMEM),
        scratch_shapes=[
            pltpu.VMEM((2, n_rows // 2, width), HALF),
            pltpu.VMEM((3, n_mark, n_rows // 2), HALF),
            pltpu.VMEM((n_query, width), HALF),
            pltpu.VMEM((n_mark, width), HALF),
            pltpu.VMEM((2, *whitening.shape), HALF),
            pltpu.SemaphoreType.DMA((parts + 3,)),
            pltpu.VMEM((n_hub, rows, n_mark), HALF),
            pltpu.VMEM((n_hub, rows, n_mark), HALF),
            pltpu.VMEM((n_layer + 2, n_land // 2, rows, n_mark), HALF),
            pltpu.VMEM((rows, n_mark), HALF),
            pltpu.VMEM((n_hub, n_land // 2, rows, n_mark), HALF),
            pltpu.VMEM((2, n_query // 2, n_mark), HALF),
            pltpu.VMEM((n_layer // 2, n_land, share, each), HALF),
            pltpu.VMEM((n_layer, n_land // 2, share, each), HALF),
            pltpu.SemaphoreType.DMA((n_hub, n_land // 2)),
            pltpu.SemaphoreType.DMA((n_layer + 2, n_land // 2)),
            pltpu.SemaphoreType.DMA((n_layer, n_land // 2)),
            pltpu.SemaphoreType.DMA((n_hub, n_land // 2)),
            pltpu.SemaphoreType.DMA((n_layer // 2, n_land)),
            pltpu.SemaphoreType.DMA((n_layer, n_land // 2)),
            pltpu.SemaphoreType.DMA((n_hub + 1,)),
            pltpu.SemaphoreType.DMA((n_hub + 1,)),
            pltpu.SemaphoreType.DMA((2,)),
            pltpu.SemaphoreType.DMA((2,)),
            pltpu.SemaphoreType.DMA((STEPS,)),
            pltpu.SemaphoreType.DMA((STEPS,)),
        ],
        compiler_params=pltpu.CompilerParams(
            collective_id=0, has_side_effects=True, vmem_limit_bytes=VMEM_LIMIT
        ),
    )(gradients.reshape(2, n_rows // 2, width), queries, landmarks, whitening)


def staged(gradients, queries, landmarks, whitening):
    factor = landmarks.shape[0] ** (-0.5)
    partial = dot(queries, landmarks, NT).astype(HALF)
    query_proj = lax.psum(partial, ("layer", "land"))
    query_white = dot(query_proj, whitening, NN).astype(HALF)
    back = lax.psum(dot(query_white, whitening, NT).astype(HALF), "land")
    spread = dot(back, landmarks, NN).astype(HALF)
    scores = dot(spread, gradients, NT) * factor
    share = lax.psum_scatter(
        scores.astype(HALF), "layer", scatter_dimension=1, tiled=True
    )
    return lax.psum_scatter(share, "land", scatter_dimension=0, tiled=True).astype(FULL)


def local(gradients, queries, landmarks, whitening):
    held = 2 * (gradients.size + queries.size + landmarks.size + whitening.size)
    here = lax.axis_size("layer") == LAYERS and lax.axis_size("land") == LANDS
    even = (
        gradients.shape[1] % (128 * PARTS) == 0
        and landmarks.shape[0] % 256 == 0
        and gradients.shape[0] % LAYERS == 0
        and queries.shape[0] == 8 * LANDS
    )
    if here and even and held <= (24 << 20):
        return fused(gradients, queries, landmarks, whitening)
    return staged(gradients, queries, landmarks, whitening)


def solution(mesh):
    return jax.shard_map(
        local,
        mesh=mesh,
        in_specs=(
            P(None, ("layer", "land")),
            P(None, ("layer", "land")),
            P(None, ("layer", "land")),
            P(None, "land"),
        ),
        out_specs=P("land", "layer"),
        check_vma=False,
    )
```
